32 devices in a mesh: row: 16 (over z, y, x), col: 2 (over core).
Axes of the slice: x: 2, y: 2, z: 4, core: 2. Of those that a mesh axis runs over, the one named last changes fastest.
Arguments:
- features: bfloat16 [8192, 128], P(('row', 'col')), may hold values from -6 to 6
- weight: bfloat16 [128, 256], replicated, may hold values from -0.5 to 0.5
- bias: float32 [256], replicated, may hold values from -3 to 3
- grad_out: bfloat16 [8192, 256], P(('row', 'col')), may hold values from -6 to 6
- tiles: bfloat16 [32, 128, 128, 128], P(('row', 'col')), may hold values from -0.25 to 0.25
- tile_count: int32 [32], P(('row', 'col')), may hold values from 1 to 128, as said below
- tile_dst: int32 [32, 128], P(('row', 'col')), may hold values from 0 to 3
- tile_src: int32 [32, 128], P(('row', 'col')), may hold values from 0 to 9
Outputs:
- activations: bfloat16 [8192, 256], P(('row', 'col'))
- grad_features: bfloat16 [8192, 128], P(('row', 'col'))
- grad_weight: float32 [128, 256], replicated
- grad_bias: float32 [256], replicated
The draws below stay inside these ranges and needn't reach their ends.
Inputs may be any that keep to these rules, and one draw needn't show every extreme that they name: Slots from tile_count on are ignored; some device holds 128 live slots.
All inputs are finite; a program needn't handle non-finite values.
Results may differ from the reference program's by a relative error of at most 0.019.
Values may be sent and summed in bfloat16 or wider, within the bound.
A program may use at most 64 MiB of HBM per device.

```python
import math
import jax
import jax.numpy as jnp
from jax import lax

F = 128
H = 256
TILE = 128
BAND = 2
NODE_DEV = 256
MAXT = 128
DST_TILES = 4
WINDOW = 10
NODES = 8192
N_ROW = 16
N_COL = 2
DEVICES = 32


def draw_tile_count(key, part):
    first, second = jax.random.split(key)
    level = jax.random.randint(first, (DEVICES,), 0, 4)
    counts = jnp.maximum(MAXT // (1 + level), 1)
    chosen = jax.random.randint(second, (), 0, DEVICES)
    counts = jnp.where(jnp.arange(DEVICES) == chosen, MAXT, counts)
    return counts.astype(jnp.int32)


def with_ends(array, own_key, low, largest):
    dims = array.shape
    place = [jax.random.randint(jax.random.fold_in(own_key, axis), (), 0, dims[axis]) for axis in range(len(dims))]
    array = array.at[tuple(place)].set(low)
    longest = dims.index(max(dims))
    place[longest] = (place[longest] + 1) % dims[longest]
    return array.at[tuple(place)].set(largest)


def levels(rng, extent, cuts, smallest, high):
    level, own = 1.0, jax.random.fold_in(rng, 6)
    for position, shards_of in cuts:
        heights = jnp.exp(jax.random.uniform(jax.random.fold_in(own, position), (shards_of,), jnp.float32, smallest / len(cuts), high / len(cuts)))
        level = level * jnp.repeat(heights, extent[position] // shards_of).reshape([-1 if axis == position else 1 for axis in range(len(extent))])
    return level


def scatter_about(own_key, dims, spread, limit, pieces=(), held_as=jnp.bfloat16):
    gain = levels(own_key, dims, pieces, -0.22, 0.18) if pieces else 1.0
    array = jax.random.normal(own_key, dims, jnp.float32) * spread * gain
    return jnp.minimum(jnp.maximum(array, -limit), limit).astype(held_as)


def setup_inputs(seed: int = 0) -> dict:
    keys = jax.random.split(jax.random.key(seed), 9)
    return {
        "features": scatter_about(keys[0], (NODES, F), 1.0, 6.0, ((0, 32),)),
        "weight": scatter_about(keys[1], (F, H), F ** -0.5, 0.5),
        "bias": scatter_about(keys[2], (H,), 0.5, 3.0, (), jnp.float32),
        "grad_out": scatter_about(keys[3], (NODES, H), 1.0, 6.0, ((0, 32),)),
        "tiles": scatter_about(keys[4], (DEVICES, MAXT, TILE, TILE), (4 * TILE) ** -0.5, 0.25, ((0, 32),)),
        "tile_count": draw_tile_count(jax.random.fold_in(keys[8], 71), 0),
        "tile_dst": with_ends(jax.random.randint(keys[6], (DEVICES, MAXT), 0, DST_TILES), jax.random.fold_in(keys[6], 1), 0, DST_TILES - 1).astype(jnp.int32),
        "tile_src": with_ends(jax.random.randint(keys[7], (DEVICES, MAXT), 0, WINDOW), jax.random.fold_in(keys[7], 1), 0, WINDOW - 1).astype(jnp.int32),
    }


def reference(features, weight, bias, grad_out, tiles, tile_count, tile_dst, tile_src):
    feat_rows = features.reshape(N_ROW, N_COL, NODE_DEV, F)
    offsets = jnp.arange(-BAND, BAND + 1, dtype=jnp.int32)
    tile_grid = tiles.reshape(N_ROW, N_COL, MAXT, TILE, TILE)
    dst_grid = tile_dst.reshape(N_ROW, N_COL, MAXT)
    src_grid = tile_src.reshape(N_ROW, N_COL, MAXT)
    count_grid = tile_count.reshape(N_ROW, N_COL)
    slots = jnp.arange(MAXT, dtype=jnp.int32)

    def forward_row(rowid):
        rows = (rowid + offsets) % N_ROW
        window = jnp.transpose(feat_rows[rows], (1, 0, 2, 3)).reshape(N_COL, WINDOW, TILE, F)

        def single(win_c, tile_c, dst_c, src_c, count_c):
            live = (slots < count_c).astype(jnp.float32)
            prod = jnp.einsum('kij,kjh->kih', tile_c.astype(jnp.float32), win_c[src_c].astype(jnp.float32))
            prod = prod * live[:, None, None]
            part = jnp.zeros((DST_TILES, TILE, F), jnp.float32).at[dst_c].add(prod)
            part = lax.optimization_barrier(part.astype(jnp.bfloat16))
            return part.astype(jnp.float32)
        parts = jax.vmap(single)(window, tile_grid[rowid], dst_grid[rowid], src_grid[rowid], count_grid[rowid])
        return lax.optimization_barrier(jnp.sum(parts, 0)).reshape(DST_TILES * TILE, F)
    aggregated = lax.map(forward_row, jnp.arange(N_ROW, dtype=jnp.int32)).reshape(NODES, F).astype(jnp.bfloat16)
    pre = jnp.dot(aggregated, weight, preferred_element_type=jnp.float32) + bias
    sig = jax.nn.sigmoid(pre)
    activations = (pre * sig).astype(jnp.bfloat16)
    dpre = (grad_out.astype(jnp.float32) * sig * (1.0 + pre * (1.0 - sig))).astype(jnp.bfloat16)
    scale = math.sqrt(NODES)
    grad_bias = lax.optimization_barrier(jnp.sum(dpre.astype(jnp.float32), 0)) / scale
    grad_weight = jnp.dot(aggregated.T, dpre, preferred_element_type=jnp.float32) / scale
    grad_agg = jnp.dot(dpre, weight.T, preferred_element_type=jnp.float32).astype(jnp.bfloat16)
    dblocks = grad_agg.reshape(N_ROW, DST_TILES, TILE, F)

    def back_row(carry, rowid):
        block = dblocks[rowid]

        def single(tile_c, dst_c, src_c, count_c):
            live = (slots < count_c).astype(jnp.float32)
            contrib = jnp.einsum('kji,kjh->kih', tile_c.astype(jnp.float32), block[dst_c].astype(jnp.float32))
            contrib = contrib * live[:, None, None]
            return jnp.zeros((WINDOW, TILE, F), jnp.float32).at[src_c].add(contrib)
        backs = jax.vmap(single)(tile_grid[rowid], dst_grid[rowid], src_grid[rowid], count_grid[rowid])
        backs = jnp.transpose(backs.reshape(N_COL, 2 * BAND + 1, NODE_DEV, F), (1, 0, 2, 3))
        rows = (rowid + offsets) % N_ROW
        return (carry.at[rows].add(backs), None)
    start = jnp.zeros((N_ROW, N_COL, NODE_DEV, F), jnp.float32)
    total, unused = lax.scan(back_row, start, jnp.arange(N_ROW, dtype=jnp.int32))
    grad_features = total.reshape(NODES, F).astype(jnp.bfloat16)
    return (activations, grad_features, grad_weight, grad_bias)
```

```python
import functools
import math

import jax
import jax.numpy as jnp
from jax import lax
from jax.experimental import pallas as pl
from jax.experimental.pallas import tpu as pltpu
from jax.sharding import PartitionSpec as P

MESH = pl.DeviceIdType.MESH
BAND = 2
OFFSETS = tuple(o for o in range(-BAND, BAND + 1) if o)
CHAINS = 2
CHUNKS = 4
F32 = jnp.float32
BF16 = jnp.bfloat16


def dot(a, b, dims):
    return lax.dot_general(a, b, (dims, ((), ())), preferred_element_type=F32)


def kernel(
    n_row, n_col, scale,
    features, weight, bias, grad_out, tiles, count, dst, src,
    act_out, gf_out, gw_out, gb_out,
    tiles_v, sums, feat_w, wt_v, bias_v, go_v, dst_v, src_v, idx_v, idx_s,
    adj, adj_t, acc, part, part_in, agg_v, dpre_v, act_v, grads, back, back_in, gf_v,
    pay, pay_in, bf_out, bf_in, gw_v, gb_v,
    tile_sem, in_sem, idx_sem, out_sem,
    halo_s, halo_r, part_s, part_r, ga_s, ga_r, bk_s, bk_r, pay_s, pay_r, bf_s, bf_r, ag_s, ag_r,
):
    row = lax.axis_index("row")
    col = lax.axis_index("col")
    node_dev, width = features.shape
    maxt, tile = tiles.shape[1], tiles.shape[2]
    window_tiles = (2 * BAND + 1) * (node_dev // tile)
    dst_tiles = n_col * node_dev // tile
    half = maxt // CHAINS
    group = half // CHUNKS
    steps = bf_out.shape[0]
    w_rows = width // n_col

    def at_row(offset):
        return {"row": lax.rem(row + offset + n_row, n_row)}

    def flip(step):
        bit = 1 << step
        up = lax.rem(row // bit, 2)
        return {"row": row + bit - 2 * bit * up}

    def clamp(index):
        return jnp.minimum(jnp.maximum(index, 0), half)

    def at_col(offset):
        return {"col": lax.rem(col + offset, n_col)}

    barrier = pltpu.get_barrier_semaphore()
    partners = (
        [at_row(o) for o in OFFSETS]
        + [flip(s) for s in range(steps)]
        + [at_col(o) for o in range(1, n_col)]
    )
    for partner in partners:
        pl.semaphore_signal(barrier, inc=1, device_id=partner, device_id_type=MESH)

    small = [
        pltpu.make_async_copy(a, b, in_sem.at[n])
        for n, (a, b) in enumerate(
            [
                (dst, dst_v),
                (src, src_v),
                (features, feat_w.at[pl.ds(BAND * node_dev, node_dev)]),
                (weight, wt_v),
                (bias, bias_v),
                (grad_out, go_v),
            ]
        )
    ]
    for copy in small[:2]:
        copy.start()
    loads = []
    for g in range(CHUNKS):
        for h in range(CHAINS):
            at = pl.ds(h * half + g * group, group)
            copy = pltpu.make_async_copy(tiles.at[0, at], tiles_v.at[at], tile_sem.at[g * CHAINS + h])
            copy.start()
            loads.append(copy)
    for copy in small[2:]:
        copy.start()

    small[0].wait()
    small[1].wait()
    lane = lax.broadcasted_iota(jnp.int32, (1, maxt), 1)
    key = jnp.where(lane < count[0], dst_v[...] * window_tiles + src_v[...], -1).astype(F32)
    key = jnp.broadcast_to(key, (maxt, maxt))
    key_t = key.T
    ri = lax.broadcasted_iota(jnp.int32, (maxt, maxt), 0)
    ci = lax.broadcasted_iota(jnp.int32, (maxt, maxt), 1)
    ri_f = ri.astype(F32)
    prev = jnp.zeros((maxt, maxt), F32)
    for h in range(CHAINS):
        inside = (ri >= h * half) & (ri < ci) & (ci < (h + 1) * half)
        prev = jnp.where((key == key_t) & inside, ri_f + (1.0 - h * half), prev)
    idx_v[0:1, 0:maxt] = jnp.max(prev, 0, keepdims=True).astype(jnp.int32)
    pairs = idx_v.shape[1]
    key_c = jnp.broadcast_to(key_t[:, 0:1], (maxt, pairs))
    pc = lax.broadcasted_iota(jnp.int32, (maxt, pairs), 1).astype(F32)
    pr = lax.broadcasted_iota(jnp.int32, (maxt, pairs), 0)
    for h in range(CHAINS):
        inside = (pr >= h * half) & (pr < (h + 1) * half)
        last = jnp.where((key_c == pc) & inside, pr.astype(F32) + (1.0 - h * half), 0.0)
        idx_v[h + 1 : h + 2, :] = jnp.max(last, 0, keepdims=True).astype(jnp.int32)
    to_scalar = pltpu.make_async_copy(idx_v, idx_s, idx_sem)
    to_scalar.start()

    pl.semaphore_wait(barrier, len(partners))
    halos = []
    for n, o in enumerate(OFFSETS):
        copy = pltpu.make_async_remote_copy(
            src_ref=features,
            dst_ref=feat_w.at[pl.ds((o + BAND) * node_dev, node_dev)],
            send_sem=halo_s.at[n],
            recv_sem=halo_r.at[n],
            device_id=at_row(-o),
            device_id_type=MESH,
        )
        copy.start()
        halos.append(copy)

    for h in range(CHAINS):
        sums[h, 0] = jnp.zeros((tile, tile), F32)
    to_scalar.wait()
    for g in range(CHUNKS):
        for h in range(CHAINS):
            loads[g * CHAINS + h].wait()

        def add(i, carry):
            slot = g * group + i
            for h in range(CHAINS):
                before = clamp(idx_s[0, h * half + slot])
                sums[h, slot + 1] = tiles_v[h * half + slot].astype(F32) + sums[h, before]
            return carry

        lax.fori_loop(0, group, add, 0, unroll=2)

    def place(j, carry):
        cols = pl.ds(pl.multiple_of(j * tile, tile), tile)
        for d in range(dst_tiles):
            total = sums[0, clamp(idx_s[1, d * window_tiles + j])]
            for h in range(1, CHAINS):
                total = total + sums[h, clamp(idx_s[h + 1, d * window_tiles + j])]
            adj[pl.ds(d * tile, tile), cols] = total.astype(BF16)
            adj_t[cols, pl.ds(d * tile, tile)] = total.T.astype(BF16)
        return carry

    lax.fori_loop(0, window_tiles, place, 0)

    for copy in small[2:]:
        copy.wait()

    def window_part(o):
        at = pl.ds((o + BAND) * node_dev, node_dev)
        return dot(adj[:, at], feat_w[at, :], ((1,), (0,)))

    acc[...] = window_part(0)
    for n, o in sorted(enumerate(OFFSETS), key=lambda p: abs(p[1])):
        halos[n].wait_recv()
        acc[...] += window_part(o)
    part[...] = acc[...].astype(BF16)

    mine = pl.ds(pl.multiple_of(col * node_dev, node_dev), node_dev)
    sends = []
    for o in range(1, n_col):
        q = lax.rem(col + o, n_col)
        copy = pltpu.make_async_remote_copy(
            src_ref=part.at[pl.ds(pl.multiple_of(q * node_dev, node_dev), node_dev)],
            dst_ref=part_in.at[col],
            send_sem=part_s.at[o - 1],
            recv_sem=part_r.at[o - 1],
            device_id=at_col(o),
            device_id_type=MESH,
        )
        copy.start()
        sends.append(copy)
    part_in[col] = part[mine, :]
    for copy in sends:
        copy.wait_recv()
    summed = part_in[0].astype(F32)
    for q in range(1, n_col):
        summed = summed + part_in[q].astype(F32)
    agg_v[...] = summed.astype(BF16)

    pre = dot(agg_v[...], wt_v[...], ((1,), (0,))) + bias_v[...]
    sig = jax.nn.sigmoid(pre)
    act_v[...] = (pre * sig).astype(BF16)
    dpre_v[...] = (go_v[...].astype(F32) * sig * (1.0 + pre * (1.0 - sig))).astype(BF16)
    grads[mine, :] = dot(dpre_v[...], wt_v[...], ((1,), (1,))).astype(BF16)
    gathers = []
    for o in range(1, n_col):
        copy = pltpu.make_async_remote_copy(
            src_ref=grads.at[mine],
            dst_ref=grads.at[mine],
            send_sem=ga_s.at[o - 1],
            recv_sem=ga_r.at[o - 1],
            device_id=at_col(o),
            device_id_type=MESH,
        )
        copy.start()
        gathers.append(copy)
    act_copy = pltpu.make_async_copy(act_v, act_out, out_sem.at[0])
    act_copy.start()

    w_term = dot(agg_v[...], dpre_v[...], ((0,), (0,))).astype(BF16)
    b_term = jnp.sum(dpre_v[...].astype(F32), 0, keepdims=True).astype(BF16)
    b_rows = pay.shape[1] - w_rows
    for q in range(n_col):
        pay[q, 0:w_rows, :] = w_term[q * w_rows : (q + 1) * w_rows, :]
        pay[q, w_rows:, :] = jnp.broadcast_to(b_term, (b_rows, b_term.shape[1]))
    pays = []
    for o in range(1, n_col):
        copy = pltpu.make_async_remote_copy(
            src_ref=pay.at[lax.rem(col + o, n_col)],
            dst_ref=pay_in.at[col],
            send_sem=pay_s.at[o - 1],
            recv_sem=pay_r.at[o - 1],
            device_id=at_col(o),
            device_id_type=MESH,
        )
        copy.start()
        pays.append(copy)
    pay_in[col] = pay[col]

    for copy in gathers:
        copy.wait_recv()

    def back_part(o):
        return dot(adj_t[pl.ds((o + BAND) * node_dev, node_dev), :], grads[...], ((1,), (0,)))

    backs = []
    for n, o in enumerate(OFFSETS):
        back[n] = back_part(o).astype(BF16)
        copy = pltpu.make_async_remote_copy(
            src_ref=back.at[n],
            dst_ref=back_in.at[n],
            send_sem=bk_s.at[n],
            recv_sem=bk_r.at[n],
            device_id=at_row(o),
            device_id_type=MESH,
        )
        copy.start()
        backs.append(copy)

    for copy in pays:
        copy.wait_recv()
    value = pay_in[0].astype(F32)
    for q in range(1, n_col):
        value = value + pay_in[q].astype(F32)
    flips = []
    for s in range(steps):
        bf_out[s] = value.astype(BF16)
        copy = pltpu.make_async_remote_copy(
            src_ref=bf_out.at[s],
            dst_ref=bf_in.at[s],
            send_sem=bf_s.at[s],
            recv_sem=bf_r.at[s],
            device_id=flip(s),
            device_id_type=MESH,
        )
        copy.start()
        flips.append(copy)
        if s == 0:
            acc[0:node_dev, :] = back_part(0)
        copy.wait_recv()
        value = bf_out[s].astype(F32) + bf_in[s].astype(F32)
    value = value * (1.0 / scale)
    w_mine = pl.ds(pl.multiple_of(col * w_rows, w_rows), w_rows)
    gw_v[w_mine, :] = value[0:w_rows, :]
    ends = []
    for o in range(1, n_col):
        copy = pltpu.make_async_remote_copy(
            src_ref=gw_v.at[w_mine],
            dst_ref=gw_v.at[w_mine],
            send_sem=ag_s.at[o - 1],
            recv_sem=ag_r.at[o - 1],
            device_id=at_col(o),
            device_id_type=MESH,
        )
        copy.start()
        ends.append(copy)
    gb_v[...] = value[w_rows : w_rows + 1, :]
    gb_copy = pltpu.make_async_copy(gb_v, gb_out, out_sem.at[3])
    gb_copy.start()

    for copy in backs:
        copy.wait_recv()
    total = acc[0:node_dev, :]
    for n in range(len(OFFSETS)):
        total = total + back_in[n].astype(F32)
    gf_v[...] = total.astype(BF16)
    gf_copy = pltpu.make_async_copy(gf_v, gf_out, out_sem.at[1])
    gf_copy.start()
    for copy in ends:
        copy.wait_recv()
    gw_copy = pltpu.make_async_copy(gw_v, gw_out, out_sem.at[2])
    gw_copy.start()
    for copy in halos + sends + gathers + pays + backs + flips + ends:
        copy.wait_send()
    for copy in (act_copy, gf_copy, gb_copy, gw_copy):
        copy.wait()


def local(n_row, n_col, features, weight, bias, grad_out, tiles, tile_count, tile_dst, tile_src):
    node_dev, width = features.shape
    hidden = weight.shape[1]
    maxt, tile = tiles.shape[1], tiles.shape[2]
    window = (2 * BAND + 1) * node_dev
    nodes = n_col * node_dev
    pairs = (nodes // tile) * (window // tile)
    pairs = max(-(-pairs // 128) * 128, maxt)
    steps = n_row.bit_length() - 1
    pay_rows = width // n_col + 16
    offs = len(OFFSETS)
    dma = pltpu.SemaphoreType.DMA
    any_spec = pl.BlockSpec(memory_space=pl.ANY)
    out = pl.pallas_call(
        functools.partial(kernel, n_row, n_col, math.sqrt(node_dev * n_row * n_col)),
        out_shape=(
            jax.ShapeDtypeStruct((node_dev, hidden), BF16),
            jax.ShapeDtypeStruct((node_dev, width), BF16),
            jax.ShapeDtypeStruct((width, hidden), F32),
            jax.ShapeDtypeStruct((1, hidden), F32),
        ),
        in_specs=[any_spec] * 5 + [pl.BlockSpec(memory_space=pltpu.SMEM)] + [any_spec] * 2,
        out_specs=(any_spec,) * 4,
        scratch_shapes=[
            pltpu.VMEM((maxt, tile, tile), BF16),
            pltpu.VMEM((CHAINS, maxt // CHAINS + 1, tile, tile), F32),
            pltpu.VMEM((window, width), BF16),
            pltpu.VMEM((width, hidden), BF16),
            pltpu.VMEM((1, hidden), F32),
            pltpu.VMEM((node_dev, hidden), BF16),
            pltpu.VMEM((1, maxt), jnp.int32),
            pltpu.VMEM((1, maxt), jnp.int32),
            pltpu.VMEM((8, pairs), jnp.int32),
            pltpu.SMEM((8, pairs), jnp.int32),
            pltpu.VMEM((nodes, window), BF16),
            pltpu.VMEM((window, nodes), BF16),
            pltpu.VMEM((nodes, width), F32),
            pltpu.VMEM((nodes, width), BF16),
            pltpu.VMEM((n_col, node_dev, width), BF16),
            pltpu.VMEM((node_dev, width), BF16),
            pltpu.VMEM((node_dev, hidden), BF16),
            pltpu.VMEM((node_dev, hidden), BF16),
            pltpu.VMEM((nodes, width), BF16),
            pltpu.VMEM((offs, node_dev, width), BF16),
            pltpu.VMEM((offs, node_dev, width), BF16),
            pltpu.VMEM((node_dev, width), BF16),
            pltpu.VMEM((n_col, pay_rows, hidden), BF16),
            pltpu.VMEM((n_col, pay_rows, hidden), BF16),
            pltpu.VMEM((steps, pay_rows, hidden), BF16),
            pltpu.VMEM((steps, pay_rows, hidden), BF16),
            pltpu.VMEM((width, hidden), F32),
            pltpu.VMEM((1, hidden), F32),
            dma((CHAINS * CHUNKS,)),
            dma((6,)),
            dma(()),
            dma((4,)),
        ]
        + [
            dma((n,))
            for n in (offs, n_col - 1, n_col - 1, offs, n_col - 1, steps, n_col - 1)
            for _ in range(2)
        ],
        compiler_params=pltpu.CompilerParams(
            collective_id=0, has_side_effects=True, vmem_limit_bytes=60 * 1024 * 1024
        ),
        name="graph_conv",
    )(features, weight, bias.reshape(1, hidden), grad_out, tiles, tile_count, tile_dst, tile_src)
    return out[0], out[1], out[2], out[3].reshape(hidden)


def solution(mesh):
    in_specs = (
        P(("row", "col"), None),
        P(),
        P(),
        P(("row", "col"), None),
        P(("row", "col"), None, None, None),
        P(("row", "col")),
        P(("row", "col"), None),
        P(("row", "col"), None),
    )
    out_specs = (P(("row", "col"), None), P(("row", "col"), None), P(), P())
    body = functools.partial(local, mesh.shape["row"], mesh.shape["col"])
    return jax.shard_map(body, mesh=mesh, in_specs=in_specs, out_specs=out_specs, check_vma=False)
```

```python
import functools
import math

import jax
import jax.numpy as jnp
from jax import lax
from jax.experimental import pallas as pl
from jax.experimental.pallas import tpu as pltpu
from jax.sharding import PartitionSpec as P

MESH = pl.DeviceIdType.MESH
BAND = 2
OFFSETS = tuple(o for o in range(-BAND, BAND + 1) if o)
CHAINS = 2
CHUNKS = 4
F32 = jnp.float32
BF16 = jnp.bfloat16


def dot(a, b, dims):
    return lax.dot_general(a, b, (dims, ((), ())), preferred_element_type=F32)


def kernel(
    n_row, n_col, scale,
    features, weight, bias, grad_out, tiles, count, dst, src,
    act_out, gf_out, gw_out, gb_out,
    tiles_v, sums, feat_w, wt_v, bias_v, go_v, dst_v, src_v, idx_v, idx_s,
    adj, adj_t, acc, part, part_in, agg_v, dpre_v, act_v, grads, back, back_in, gf_v,
    pay, pay_in, bf_out, bf_in, gw_v, gb_v,
    tile_sem, in_sem, idx_sem, out_sem,
    halo_s, halo_r, part_s, part_r, ga_s, ga_r, bk_s, bk_r, pay_s, pay_r, bf_s, bf_r, ag_s, ag_r,
):
    row = lax.axis_index("row")
    col = lax.axis_index("col")
    node_dev, width = features.shape
    maxt, tile = tiles.shape[1], tiles.shape[2]
    window_tiles = (2 * BAND + 1) * (node_dev // tile)
    dst_tiles = n_col * node_dev // tile
    half = maxt // CHAINS
    group = half // CHUNKS
    steps = bf_out.shape[0]
    w_rows = width // n_col

    def at_row(offset):
        return {"row": lax.rem(row + offset + n_row, n_row)}

    def flip(step):
        bit = 1 << step
        up = lax.rem(row // bit, 2)
        return {"row": row + bit - 2 * bit * up}

    def clamp(index):
        return jnp.minimum(jnp.maximum(index, 0), half)

    def at_col(offset):
        return {"col": lax.rem(col + offset, n_col)}

    barrier = pltpu.get_barrier_semaphore()
    partners = (
        [at_row(o) for o in OFFSETS]
        + [flip(s) for s in range(steps)]
        + [at_col(o) for o in range(1, n_col)]
    )
    for partner in partners:
        pl.semaphore_signal(barrier, inc=1, device_id=partner, device_id_type=MESH)

    small = [
        pltpu.make_async_copy(a, b, in_sem.at[n])
        for n, (a, b) in enumerate(
            [
                (dst, dst_v),
                (src, src_v),
                (features, feat_w.at[pl.ds(BAND * node_dev, node_dev)]),
                (weight, wt_v),
                (bias, bias_v),
                (grad_out, go_v),
            ]
        )
    ]
    for copy in small[:2]:
        copy.start()
    loads = []
    for g in range(CHUNKS):
        for h in range(CHAINS):
            at = pl.ds(h * half + g * group, group)
            copy = pltpu.make_async_copy(tiles.at[0, at], tiles_v.at[at], tile_sem.at[g * CHAINS + h])
            copy.start()
            loads.append(copy)
    for copy in small[2:]:
        copy.start()

    small[0].wait()
    small[1].wait()
    lane = lax.broadcasted_iota(jnp.int32, (1, maxt), 1)
    key = jnp.where(lane < count[0], dst_v[...] * window_tiles + src_v[...], -1).astype(F32)
    key = jnp.broadcast_to(key, (maxt, maxt))
    key_t = key.T
    ri = lax.broadcasted_iota(jnp.int32, (maxt, maxt), 0)
    ci = lax.broadcasted_iota(jnp.int32, (maxt, maxt), 1)
    ri_f = ri.astype(F32)
    prev = jnp.zeros((maxt, maxt), F32)
    for h in range(CHAINS):
        inside = (ri >= h * half) & (ri < ci) & (ci < (h + 1) * half)
        prev = jnp.where((key == key_t) & inside, ri_f + (1.0 - h * half), prev)
    idx_v[0:1, 0:maxt] = jnp.max(prev, 0, keepdims=True).astype(jnp.int32)
    pairs = idx_v.shape[1]
    key_c = jnp.broadcast_to(key_t[:, 0:1], (maxt, pairs))
    pc = lax.broadcasted_iota(jnp.int32, (maxt, pairs), 1).astype(F32)
    pr = lax.broadcasted_iota(jnp.int32, (maxt, pairs), 0)
    for h in range(CHAINS):
        inside = (pr >= h * half) & (pr < (h + 1) * half)
        last = jnp.where((key_c == pc) & inside, pr.astype(F32) + (1.0 - h * half), 0.0)
        idx_v[h + 1 : h + 2, :] = jnp.max(last, 0, keepdims=True).astype(jnp.int32)
    to_scalar = pltpu.make_async_copy(idx_v, idx_s, idx_sem)
    to_scalar.start()

    pl.semaphore_wait(barrier, len(partners))
    halos = []
    for n, o in enumerate(OFFSETS):
        copy = pltpu.make_async_remote_copy(
            src_ref=features,
            dst_ref=feat_w.at[pl.ds((o + BAND) * node_dev, node_dev)],
            send_sem=halo_s.at[n],
            recv_sem=halo_r.at[n],
            device_id=at_row(-o),
            device_id_type=MESH,
        )
        copy.start()
        halos.append(copy)

    for h in range(CHAINS):
        sums[h, 0] = jnp.zeros((tile, tile), F32)
    to_scalar.wait()
    for g in range(CHUNKS):
        for h in range(CHAINS):
            loads[g * CHAINS + h].wait()

        def add(i, carry):
            slot = g * group + i
            for h in range(CHAINS):
                before = clamp(idx_s[0, h * half + slot])
                sums[h, slot + 1] = tiles_v[h * half + slot].astype(F32) + sums[h, before]
            return carry

        lax.fori_loop(0, group, add, 0, unroll=2)

    def place(j, carry):
        cols = pl.ds(pl.multiple_of(j * tile, tile), tile)
        for d in range(dst_tiles):
            total = sums[0, clamp(idx_s[1, d * window_tiles + j])]
            for h in range(1, CHAINS):
                total = total + sums[h, clamp(idx_s[h + 1, d * window_tiles + j])]
            adj[pl.ds(d * tile, tile), cols] = total.astype(BF16)
            adj_t[cols, pl.ds(d * tile, tile)] = total.T.astype(BF16)
        return carry

    lax.fori_loop(0, window_tiles, place, 0)

    for copy in small[2:]:
        copy.wait()

    def window_part(o):
        at = pl.ds((o + BAND) * node_dev, node_dev)
        return dot(adj[:, at], feat_w[at, :], ((1,), (0,)))

    acc[...] = window_part(0)
    for n, o in sorted(enumerate(OFFSETS), key=lambda p: abs(p[1])):
        halos[n].wait_recv()
        acc[...] += window_part(o)
    part[...] = acc[...].astype(BF16)

    mine = pl.ds(pl.multiple_of(col * node_dev, node_dev), node_dev)
    sends = []
    for o in range(1, n_col):
        q = lax.rem(col + o, n_col)
        copy = pltpu.make_async_remote_copy(
            src_ref=part.at[pl.ds(pl.multiple_of(q * node_dev, node_dev), node_dev)],
            dst_ref=part_in.at[col],
            send_sem=part_s.at[o - 1],
            recv_sem=part_r.at[o - 1],
            device_id=at_col(o),
            device_id_type=MESH,
        )
        copy.start()
        sends.append(copy)
    part_in[col] = part[mine, :]
    for copy in sends:
        copy.wait_recv()
    summed = part_in[0].astype(F32)
    for q in range(1, n_col):
        summed = summed + part_in[q].astype(F32)
    agg_v[...] = summed.astype(BF16)

    pre = dot(agg_v[...], wt_v[...], ((1,), (0,))) + bias_v[...]
    sig = jax.nn.sigmoid(pre)
    act_v[...] = (pre * sig).astype(BF16)
    dpre_v[...] = (go_v[...].astype(F32) * sig * (1.0 + pre * (1.0 - sig))).astype(BF16)
    w_term = dot(agg_v[...], dpre_v[...], ((0,), (0,))).astype(BF16)
    b_term = jnp.sum(dpre_v[...].astype(F32), 0, keepdims=True).astype(BF16)
    b_rows = pay.shape[1] - w_rows
    for q in range(n_col):
        pay[q, 0:w_rows, :] = w_term[q * w_rows : (q + 1) * w_rows, :]
        pay[q, w_rows:, :] = jnp.broadcast_to(b_term, (b_rows, b_term.shape[1]))
    pays = []
    for o in range(1, n_col):
        copy = pltpu.make_async_remote_copy(
            src_ref=pay.at[lax.rem(col + o, n_col)],
            dst_ref=pay_in.at[col],
            send_sem=pay_s.at[o - 1],
            recv_sem=pay_r.at[o - 1],
            device_id=at_col(o),
            device_id_type=MESH,
        )
        copy.start()
        pays.append(copy)
    pay_in[col] = pay[col]

    grads[mine, :] = dot(dpre_v[...], wt_v[...], ((1,), (1,))).astype(BF16)
    gathers = []
    for o in range(1, n_col):
        copy = pltpu.make_async_remote_copy(
            src_ref=grads.at[mine],
            dst_ref=grads.at[mine],
            send_sem=ga_s.at[o - 1],
            recv_sem=ga_r.at[o - 1],
            device_id=at_col(o),
            device_id_type=MESH,
        )
        copy.start()
        gathers.append(copy)
    act_copy = pltpu.make_async_copy(act_v, act_out, out_sem.at[0])
    act_copy.start()

    for copy in gathers:
        copy.wait_recv()

    def back_part(o):
        return dot(adj_t[pl.ds((o + BAND) * node_dev, node_dev), :], grads[...], ((1,), (0,)))

    backs = []
    for n, o in enumerate(OFFSETS):
        back[n] = back_part(o).astype(BF16)
        copy = pltpu.make_async_remote_copy(
            src_ref=back.at[n],
            dst_ref=back_in.at[n],
            send_sem=bk_s.at[n],
            recv_sem=bk_r.at[n],
            device_id=at_row(o),
            device_id_type=MESH,
        )
        copy.start()
        backs.append(copy)

    for copy in pays:
        copy.wait_recv()
    value = pay_in[0].astype(F32)
    for q in range(1, n_col):
        value = value + pay_in[q].astype(F32)
    flips = []
    for s in range(steps):
        bf_out[s] = value.astype(BF16)
        copy = pltpu.make_async_remote_copy(
            src_ref=bf_out.at[s],
            dst_ref=bf_in.at[s],
            send_sem=bf_s.at[s],
            recv_sem=bf_r.at[s],
            device_id=flip(s),
            device_id_type=MESH,
        )
        copy.start()
        flips.append(copy)
        if s == 0:
            acc[0:node_dev, :] = back_part(0)
        copy.wait_recv()
        value = bf_out[s].astype(F32) + bf_in[s].astype(F32)
    value = value * (1.0 / scale)
    w_mine = pl.ds(pl.multiple_of(col * w_rows, w_rows), w_rows)
    gw_v[w_mine, :] = value[0:w_rows, :]
    ends = []
    for o in range(1, n_col):
        copy = pltpu.make_async_remote_copy(
            src_ref=gw_v.at[w_mine],
            dst_ref=gw_v.at[w_mine],
            send_sem=ag_s.at[o - 1],
            recv_sem=ag_r.at[o - 1],
            device_id=at_col(o),
            device_id_type=MESH,
        )
        copy.start()
        ends.append(copy)
    gb_v[...] = value[w_rows : w_rows + 1, :]
    gb_copy = pltpu.make_async_copy(gb_v, gb_out, out_sem.at[3])
    gb_copy.start()

    for copy in backs:
        copy.wait_recv()
    total = acc[0:node_dev, :]
    for n in range(len(OFFSETS)):
        total = total + back_in[n].astype(F32)
    gf_v[...] = total.astype(BF16)
    gf_copy = pltpu.make_async_copy(gf_v, gf_out, out_sem.at[1])
    gf_copy.start()
    for copy in ends:
        copy.wait_recv()
    gw_copy = pltpu.make_async_copy(gw_v, gw_out, out_sem.at[2])
    gw_copy.start()
    for copy in halos + sends + gathers + pays + backs + flips + ends:
        copy.wait_send()
    for copy in (act_copy, gf_copy, gb_copy, gw_copy):
        copy.wait()


def finish(act_in, gf_in, gw_in, gb_in, act_out, gf_out, gw_out, gb_out):
    act_out[...] = act_in[...]
    gf_out[...] = gf_in[...]
    gw_out[...] = gw_in[...]
    gb_out[...] = gb_in[...]


def local(n_row, n_col, features, weight, bias, grad_out, tiles, tile_count, tile_dst, tile_src):
    node_dev, width = features.shape
    hidden = weight.shape[1]
    maxt, tile = tiles.shape[1], tiles.shape[2]
    window = (2 * BAND + 1) * node_dev
    nodes = n_col * node_dev
    pairs = (nodes // tile) * (window // tile)
    pairs = max(-(-pairs // 128) * 128, maxt)
    steps = n_row.bit_length() - 1
    pay_rows = width // n_col + 16
    offs = len(OFFSETS)
    dma = pltpu.SemaphoreType.DMA
    any_spec = pl.BlockSpec(memory_space=pl.ANY)
    out = pl.pallas_call(
        functools.partial(kernel, n_row, n_col, math.sqrt(node_dev * n_row * n_col)),
        out_shape=(
            jax.ShapeDtypeStruct((node_dev, hidden), BF16),
            jax.ShapeDtypeStruct((node_dev, width), BF16),
            jax.ShapeDtypeStruct((width, hidden), F32),
            jax.ShapeDtypeStruct((1, hidden), F32),
        ),
        in_specs=[any_spec] * 5 + [pl.BlockSpec(memory_space=pltpu.SMEM)] + [any_spec] * 2,
        out_specs=(any_spec,) * 4,
        scratch_shapes=[
            pltpu.VMEM((maxt, tile, tile), BF16),
            pltpu.VMEM((CHAINS, maxt // CHAINS + 1, tile, tile), F32),
            pltpu.VMEM((window, width), BF16),
            pltpu.VMEM((width, hidden), BF16),
            pltpu.VMEM((1, hidden), F32),
            pltpu.VMEM((node_dev, hidden), BF16),
            pltpu.VMEM((1, maxt), jnp.int32),
            pltpu.VMEM((1, maxt), jnp.int32),
            pltpu.VMEM((8, pairs), jnp.int32),
            pltpu.SMEM((8, pairs), jnp.int32),
            pltpu.VMEM((nodes, window), BF16),
            pltpu.VMEM((window, nodes), BF16),
            pltpu.VMEM((nodes, width), F32),
            pltpu.VMEM((nodes, width), BF16),
            pltpu.VMEM((n_col, node_dev, width), BF16),
            pltpu.VMEM((node_dev, width), BF16),
            pltpu.VMEM((node_dev, hidden), BF16),
            pltpu.VMEM((node_dev, hidden), BF16),
            pltpu.VMEM((nodes, width), BF16),
            pltpu.VMEM((offs, node_dev, width), BF16),
            pltpu.VMEM((offs, node_dev, width), BF16),
            pltpu.VMEM((node_dev, width), BF16),
            pltpu.VMEM((n_col, pay_rows, hidden), BF16),
            pltpu.VMEM((n_col, pay_rows, hidden), BF16),
            pltpu.VMEM((steps, pay_rows, hidden), BF16),
            pltpu.VMEM((steps, pay_rows, hidden), BF16),
            pltpu.VMEM((width, hidden), F32),
            pltpu.VMEM((1, hidden), F32),
            dma((CHAINS * CHUNKS,)),
            dma((6,)),
            dma(()),
            dma((4,)),
        ]
        + [
            dma((n,))
            for n in (offs, n_col - 1, n_col - 1, offs, n_col - 1, steps, n_col - 1)
            for _ in range(2)
        ],
        compiler_params=pltpu.CompilerParams(
            collective_id=0, has_side_effects=True, vmem_limit_bytes=60 * 1024 * 1024
        ),
        name="graph_conv",
    )(features, weight, bias.reshape(1, hidden), grad_out, tiles, tile_count, tile_dst, tile_src)
    vmem = pl.BlockSpec(memory_space=pltpu.VMEM)
    out = pl.pallas_call(
        finish,
        out_shape=tuple(jax.ShapeDtypeStruct(o.shape, o.dtype) for o in out),
        in_specs=[vmem] * 4,
        out_specs=(vmem,) * 4,
        name="finish",
    )(*out)
    return out[0], out[1], out[2], out[3].reshape(hidden)


def solution(mesh):
    in_specs = (
        P(("row", "col"), None),
        P(),
        P(),
        P(("row", "col"), None),
        P(("row", "col"), None, None, None),
        P(("row", "col")),
        P(("row", "col"), None),
        P(("row", "col"), None),
    )
    out_specs = (P(("row", "col"), None), P(("row", "col"), None), P(), P())
    body = functools.partial(local, mesh.shape["row"], mesh.shape["col"])
    return jax.shard_map(body, mesh=mesh, in_specs=in_specs, out_specs=out_specs, check_vma=False)
```

```python
import functools
import math

import jax
import jax.numpy as jnp
from jax import lax
from jax.experimental import pallas as pl
from jax.experimental.pallas import tpu as pltpu
from jax.sharding import PartitionSpec as P

MESH = pl.DeviceIdType.MESH
BAND = 2
OFFSETS = tuple(o for o in range(-BAND, BAND + 1) if o)
CHAINS = 2
CHUNKS = 4
F32 = jnp.float32
BF16 = jnp.bfloat16


def dot(a, b, dims):
    return lax.dot_general(a, b, (dims, ((), ())), preferred_element_type=F32)


def kernel(
    n_row, n_col,
    features, weight, bias, grad_out, tiles, count, dst, src,
    act_out, gf_out, gw_out, gb_out,
    tiles_v, sums, feat_w, wt_v, bias_v, go_v, dst_v, src_v, idx_v, idx_s,
    adj, adj_t, acc, part, part_in, agg_v, dpre_v, act_v, grads, back, back_in, gf_v,
    pay, pay_in, bf_in, gw_v, gb_v,
    tile_sem, in_sem, idx_sem, out_sem,
    halo_s, halo_r, part_s, part_r, ga_s, ga_r, bk_s, bk_r, pay_s, pay_r, bf_s, bf_r, ag_s, ag_r,
):
    row = lax.axis_index("row")
    col = lax.axis_index("col")
    node_dev, width = features.shape
    maxt, tile = tiles.shape[1], tiles.shape[2]
    window_tiles = (2 * BAND + 1) * (node_dev // tile)
    dst_tiles = n_col * node_dev // tile
    half = maxt // CHAINS
    group = half // CHUNKS
    n_plane, pay_rows = pay.shape[0], pay.shape[1]
    low_n = n_plane // n_col
    high_n = n_row // low_n
    w_rows = width // n_plane
    b_at = gw_out.shape[1]

    def at_row(offset):
        return {"row": lax.rem(row + offset + n_row, n_row)}

    low, high = lax.rem(row, low_n), row // low_n
    place_id = low * n_col + col

    def in_plane(offset):
        q = lax.rem(place_id + offset, n_plane)
        return q, {"row": high * low_n + q // n_col, "col": lax.rem(q, n_col)}

    def across(offset):
        return {"row": lax.rem(high + offset, high_n) * low_n + low}

    def clamp(index):
        return jnp.minimum(jnp.maximum(index, 0), half)

    def at_col(offset):
        return {"col": lax.rem(col + offset, n_col)}

    barrier = pltpu.get_barrier_semaphore()
    partners = (
        [at_row(o) for o in OFFSETS]
        + [in_plane(o)[1] for o in range(1, n_plane)]
        + [across(o) for o in range(1, high_n)]
    )
    for partner in partners:
        pl.semaphore_signal(barrier, inc=1, device_id=partner, device_id_type=MESH)

    small = [
        pltpu.make_async_copy(a, b, in_sem.at[n])
        for n, (a, b) in enumerate(
            [
                (dst, dst_v),
                (src, src_v),
                (features, feat_w.at[pl.ds(BAND * node_dev, node_dev)]),
                (weight, wt_v),
                (bias, bias_v),
                (grad_out, go_v),
            ]
        )
    ]
    for copy in small[:2]:
        copy.start()
    loads = []
    for g in range(CHUNKS):
        for h in range(CHAINS):
            at = pl.ds(h * half + g * group, group)
            copy = pltpu.make_async_copy(tiles.at[0, at], tiles_v.at[at], tile_sem.at[g * CHAINS + h])
            copy.start()
            loads.append(copy)
    for copy in small[2:]:
        copy.start()

    small[0].wait()
    small[1].wait()
    lane = lax.broadcasted_iota(jnp.int32, (1, maxt), 1)
    key = jnp.where(lane < count[0], dst_v[...] * window_tiles + src_v[...], -1).astype(F32)
    key = jnp.broadcast_to(key, (maxt, maxt))
    key_t = key.T
    ri = lax.broadcasted_iota(jnp.int32, (maxt, maxt), 0)
    ci = lax.broadcasted_iota(jnp.int32, (maxt, maxt), 1)
    ri_f = ri.astype(F32)
    prev = jnp.zeros((maxt, maxt), F32)
    for h in range(CHAINS):
        inside = (ri >= h * half) & (ri < ci) & (ci < (h + 1) * half)
        prev = jnp.where((key == key_t) & inside, ri_f + (1.0 - h * half), prev)
    idx_v[0:1, 0:maxt] = jnp.max(prev, 0, keepdims=True).astype(jnp.int32)
    pairs = idx_v.shape[1]
    key_c = jnp.broadcast_to(key_t[:, 0:1], (maxt, pairs))
    pc = lax.broadcasted_iota(jnp.int32, (maxt, pairs), 1).astype(F32)
    pr = lax.broadcasted_iota(jnp.int32, (maxt, pairs), 0)
    for h in range(CHAINS):
        inside = (pr >= h * half) & (pr < (h + 1) * half)
        last = jnp.where((key_c == pc) & inside, pr.astype(F32) + (1.0 - h * half), 0.0)
        idx_v[h + 1 : h + 2, :] = jnp.max(last, 0, keepdims=True).astype(jnp.int32)
    to_scalar = pltpu.make_async_copy(idx_v, idx_s, idx_sem)
    to_scalar.start()

    pl.semaphore_wait(barrier, len(partners))
    halos = []
    for n, o in enumerate(OFFSETS):
        copy = pltpu.make_async_remote_copy(
            src_ref=features,
            dst_ref=feat_w.at[pl.ds((o + BAND) * node_dev, node_dev)],
            send_sem=halo_s.at[n],
            recv_sem=halo_r.at[n],
            device_id=at_row(-o),
            device_id_type=MESH,
        )
        copy.start()
        halos.append(copy)

    for h in range(CHAINS):
        sums[h, 0] = jnp.zeros((tile, tile), F32)
    to_scalar.wait()
    for g in range(CHUNKS):
        for h in range(CHAINS):
            loads[g * CHAINS + h].wait()

        def add(i, carry):
            slot = g * group + i
            for h in range(CHAINS):
                before = clamp(idx_s[0, h * half + slot])
                sums[h, slot + 1] = tiles_v[h * half + slot].astype(F32) + sums[h, before]
            return carry

        lax.fori_loop(0, group, add, 0, unroll=2)

    def place(j, carry):
        cols = pl.ds(pl.multiple_of(j * tile, tile), tile)
        for d in range(dst_tiles):
            total = sums[0, clamp(idx_s[1, d * window_tiles + j])]
            for h in range(1, CHAINS):
                total = total + sums[h, clamp(idx_s[h + 1, d * window_tiles + j])]
            adj[pl.ds(d * tile, tile), cols] = total.astype(BF16)
            adj_t[cols, pl.ds(d * tile, tile)] = total.T.astype(BF16)
        return carry

    lax.fori_loop(0, window_tiles, place, 0)

    for copy in small[2:]:
        copy.wait()

    def window_part(o):
        at = pl.ds((o + BAND) * node_dev, node_dev)
        return dot(adj[:, at], feat_w[at, :], ((1,), (0,)))

    acc[...] = window_part(0)
    for n, o in sorted(enumerate(OFFSETS), key=lambda p: abs(p[1])):
        halos[n].wait_recv()
        acc[...] += window_part(o)
    part[...] = acc[...].astype(BF16)

    mine = pl.ds(pl.multiple_of(col * node_dev, node_dev), node_dev)
    sends = []
    for o in range(1, n_col):
        q = lax.rem(col + o, n_col)
        copy = pltpu.make_async_remote_copy(
            src_ref=part.at[pl.ds(pl.multiple_of(q * node_dev, node_dev), node_dev)],
            dst_ref=part_in.at[col],
            send_sem=part_s.at[o - 1],
            recv_sem=part_r.at[o - 1],
            device_id=at_col(o),
            device_id_type=MESH,
        )
        copy.start()
        sends.append(copy)
    part_in[col] = part[mine, :]
    for copy in sends:
        copy.wait_recv()
    summed = part_in[0].astype(F32)
    for q in range(1, n_col):
        summed = summed + part_in[q].astype(F32)
    agg_v[...] = summed.astype(BF16)

    pre = dot(agg_v[...], wt_v[...], ((1,), (0,))) + bias_v[...]
    sig = jax.nn.sigmoid(pre)
    act_v[...] = (pre * sig).astype(BF16)
    dpre_v[...] = (go_v[...].astype(F32) * sig * (1.0 + pre * (1.0 - sig))).astype(BF16)
    w_term = dot(agg_v[...], dpre_v[...], ((0,), (0,))).astype(BF16)
    b_term = jnp.sum(dpre_v[...].astype(F32), 0, keepdims=True).astype(BF16)
    for q in range(n_plane):
        pay[q, 0:w_rows, :] = w_term[q * w_rows : (q + 1) * w_rows, :]
        pay[q, b_at:, :] = jnp.broadcast_to(b_term, (pay_rows - b_at, b_term.shape[1]))
    pays = []
    for o in range(1, n_plane):
        q, target = in_plane(o)
        copy = pltpu.make_async_remote_copy(
            src_ref=pay.at[q],
            dst_ref=pay_in.at[place_id],
            send_sem=pay_s.at[o - 1],
            recv_sem=pay_r.at[o - 1],
            device_id=target,
            device_id_type=MESH,
        )
        copy.start()
        pays.append(copy)
    pay_in[place_id] = pay[place_id]

    grads[mine, :] = dot(dpre_v[...], wt_v[...], ((1,), (1,))).astype(BF16)
    gathers = []
    for o in range(1, n_col):
        copy = pltpu.make_async_remote_copy(
            src_ref=grads.at[mine],
            dst_ref=grads.at[mine],
            send_sem=ga_s.at[o - 1],
            recv_sem=ga_r.at[o - 1],
            device_id=at_col(o),
            device_id_type=MESH,
        )
        copy.start()
        gathers.append(copy)
    act_copy = pltpu.make_async_copy(act_v, act_out, out_sem.at[0])
    act_copy.start()

    for copy in gathers:
        copy.wait_recv()

    def back_part(o):
        return dot(adj_t[pl.ds((o + BAND) * node_dev, node_dev), :], grads[...], ((1,), (0,)))

    backs = []
    for n, o in enumerate(OFFSETS):
        back[n] = back_part(o).astype(BF16)
        copy = pltpu.make_async_remote_copy(
            src_ref=back.at[n],
            dst_ref=back_in.at[n],
            send_sem=bk_s.at[n],
            recv_sem=bk_r.at[n],
            device_id=at_row(o),
            device_id_type=MESH,
        )
        copy.start()
        backs.append(copy)

    for copy in pays:
        copy.wait_recv()
    value = pay_in[0].astype(F32)
    for q in range(1, n_plane):
        value = value + pay_in[q].astype(F32)
    bf_in[high] = value.astype(BF16)
    flips = []
    for o in range(1, high_n):
        copy = pltpu.make_async_remote_copy(
            src_ref=bf_in.at[high],
            dst_ref=bf_in.at[high],
            send_sem=bf_s.at[o - 1],
            recv_sem=bf_r.at[o - 1],
            device_id=across(o),
            device_id_type=MESH,
        )
        copy.start()
        flips.append(copy)
    acc[0:node_dev, :] = back_part(0)
    for copy in flips:
        copy.wait_recv()
    value = bf_in[0].astype(F32)
    for q in range(1, high_n):
        value = value + bf_in[q].astype(F32)
    gw_v[place_id] = value[0:b_at, :].astype(BF16)
    ends = []
    for o in range(1, n_plane):
        copy = pltpu.make_async_remote_copy(
            src_ref=gw_v.at[place_id],
            dst_ref=gw_v.at[place_id],
            send_sem=ag_s.at[o - 1],
            recv_sem=ag_r.at[o - 1],
            device_id=in_plane(o)[1],
            device_id_type=MESH,
        )
        copy.start()
        ends.append(copy)
    gb_v[...] = value[b_at : b_at + 1, :]
    gb_copy = pltpu.make_async_copy(gb_v, gb_out, out_sem.at[3])
    gb_copy.start()

    for copy in backs:
        copy.wait_recv()
    total = acc[0:node_dev, :]
    for n in range(len(OFFSETS)):
        total = total + back_in[n].astype(F32)
    gf_v[...] = total.astype(BF16)
    gf_copy = pltpu.make_async_copy(gf_v, gf_out, out_sem.at[1])
    gf_copy.start()
    for copy in ends:
        copy.wait_recv()
    gw_copy = pltpu.make_async_copy(gw_v, gw_out, out_sem.at[2])
    gw_copy.start()
    for copy in halos + sends + gathers + pays + backs + flips + ends:
        copy.wait_send()
    for copy in (act_copy, gf_copy, gb_copy, gw_copy):
        copy.wait()


def finish(scale, act_in, gf_in, gw_in, gb_in, act_out, gf_out, gw_out, gb_out):
    act_out[...] = act_in[...]
    gf_out[...] = gf_in[...]
    rows = gw_out.shape[0] // gw_in.shape[0]
    for q in range(gw_in.shape[0]):
        gw_out[q * rows : (q + 1) * rows, :] = gw_in[q, 0:rows, :].astype(F32) * (1.0 / scale)
    gb_out[...] = gb_in[...] * (1.0 / scale)


def local(n_row, n_col, features, weight, bias, grad_out, tiles, tile_count, tile_dst, tile_src):
    node_dev, width = features.shape
    hidden = weight.shape[1]
    maxt, tile = tiles.shape[1], tiles.shape[2]
    window = (2 * BAND + 1) * node_dev
    nodes = n_col * node_dev
    pairs = (nodes // tile) * (window // tile)
    pairs = max(-(-pairs // 128) * 128, maxt)
    low_n = math.isqrt(n_row)
    while n_row % low_n:
        low_n -= 1
    high_n = n_row // low_n
    n_plane = low_n * n_col
    b_at = -(-(width // n_plane) // 8) * 8
    pay_rows = b_at + 8
    offs = len(OFFSETS)
    dma = pltpu.SemaphoreType.DMA
    any_spec = pl.BlockSpec(memory_space=pl.ANY)
    out = pl.pallas_call(
        functools.partial(kernel, n_row, n_col),
        out_shape=(
            jax.ShapeDtypeStruct((node_dev, hidden), BF16),
            jax.ShapeDtypeStruct((node_dev, width), BF16),
            jax.ShapeDtypeStruct((n_plane, b_at, hidden), BF16),
            jax.ShapeDtypeStruct((1, hidden), F32),
        ),
        in_specs=[any_spec] * 5 + [pl.BlockSpec(memory_space=pltpu.SMEM)] + [any_spec] * 2,
        out_specs=(any_spec,) * 4,
        scratch_shapes=[
            pltpu.VMEM((maxt, tile, tile), BF16),
            pltpu.VMEM((CHAINS, maxt // CHAINS + 1, tile, tile), F32),
            pltpu.VMEM((window, width), BF16),
            pltpu.VMEM((width, hidden), BF16),
            pltpu.VMEM((1, hidden), F32),
            pltpu.VMEM((node_dev, hidden), BF16),
            pltpu.VMEM((1, maxt), jnp.int32),
            pltpu.VMEM((1, maxt), jnp.int32),
            pltpu.VMEM((8, pairs), jnp.int32),
            pltpu.SMEM((8, pairs), jnp.int32),
            pltpu.VMEM((nodes, window), BF16),
            pltpu.VMEM((window, nodes), BF16),
            pltpu.VMEM((nodes, width), F32),
            pltpu.VMEM((nodes, width), BF16),
            pltpu.VMEM((n_col, node_dev, width), BF16),
            pltpu.VMEM((node_dev, width), BF16),
            pltpu.VMEM((node_dev, hidden), BF16),
            pltpu.VMEM((node_dev, hidden), BF16),
            pltpu.VMEM((nodes, width), BF16),
            pltpu.VMEM((offs, node_dev, width), BF16),
            pltpu.VMEM((offs, node_dev, width), BF16),
            pltpu.VMEM((node_dev, width), BF16),
            pltpu.VMEM((n_plane, pay_rows, hidden), BF16),
            pltpu.VMEM((n_plane, pay_rows, hidden), BF16),
            pltpu.VMEM((high_n, pay_rows, hidden), BF16),
            pltpu.VMEM((n_plane, b_at, hidden), BF16),
            pltpu.VMEM((1, hidden), F32),
            dma((CHAINS * CHUNKS,)),
            dma((6,)),
            dma(()),
            dma((4,)),
        ]
        + [
            dma((n,))
            for n in (offs, n_col - 1, n_col - 1, offs, n_plane - 1, high_n - 1, n_plane - 1)
            for _ in range(2)
        ],
        compiler_params=pltpu.CompilerParams(
            collective_id=0, has_side_effects=True, vmem_limit_bytes=60 * 1024 * 1024
        ),
        name="graph_conv",
    )(features, weight, bias.reshape(1, hidden), grad_out, tiles, tile_count, tile_dst, tile_src)
    vmem = pl.BlockSpec(memory_space=pltpu.VMEM)
    out = pl.pallas_call(
        functools.partial(finish, math.sqrt(node_dev * n_row * n_col)),
        out_shape=(
            jax.ShapeDtypeStruct((node_dev, hidden), BF16),
            jax.ShapeDtypeStruct((node_dev, width), BF16),
            jax.ShapeDtypeStruct((width, hidden), F32),
            jax.ShapeDtypeStruct((1, hidden), F32),
        ),
        in_specs=[vmem] * 4,
        out_specs=(vmem,) * 4,
        name="finish",
    )(*out)
    return out[0], out[1], out[2], out[3].reshape(hidden)


def solution(mesh):
    in_specs = (
        P(("row", "col"), None),
        P(),
        P(),
        P(("row", "col"), None),
        P(("row", "col"), None, None, None),
        P(("row", "col")),
        P(("row", "col"), None),
        P(("row", "col"), None),
    )
    out_specs = (P(("row", "col"), None), P(("row", "col"), None), P(), P())
    body = functools.partial(local, mesh.shape["row"], mesh.shape["col"])
    return jax.shard_map(body, mesh=mesh, in_specs=in_specs, out_specs=out_specs, check_vma=False)
```

```python
import functools
import math

import jax
import jax.numpy as jnp
from jax import lax
from jax.experimental import pallas as pl
from jax.experimental.pallas import tpu as pltpu
from jax.sharding import PartitionSpec as P

MESH = pl.DeviceIdType.MESH
BAND = 2
OFFSETS = tuple(o for o in range(-BAND, BAND + 1) if o)
CHAINS = 2
CHUNKS = 4
F32 = jnp.float32
BF16 = jnp.bfloat16


def dot(a, b, dims):
    return lax.dot_general(a, b, (dims, ((), ())), preferred_element_type=F32)


def kernel(
    n_row, n_col,
    features, weight, bias, grad_out, tiles, count, dst, src,
    act_out, gf_out, gw_out, gb_out,
    tiles_v, sums, feat_w, wt_v, bias_v, go_v, dst_v, src_v, idx_v, idx_s,
    adj, adj_t, acc, part, part_in, agg_v, dpre_v, act_v, grads, back, back_in, gf_v,
    pay, pay_in, bf_in, gw_v, gb_v,
    tile_sem, in_sem, idx_sem, out_sem,
    halo_s, halo_r, part_s, part_r, ga_s, ga_r, bk_s, bk_r, pay_s, pay_r, bf_s, bf_r, ag_s, ag_r,
):
    row = lax.axis_index("row")
    col = lax.axis_index("col")
    node_dev, width = features.shape
    maxt, tile = tiles.shape[1], tiles.shape[2]
    window_tiles = (2 * BAND + 1) * (node_dev // tile)
    dst_tiles = n_col * node_dev // tile
    half = maxt // CHAINS
    group = half // CHUNKS
    n_plane, pay_rows = pay.shape[0], pay.shape[1]
    low_n = n_plane // n_col
    high_n = n_row // low_n
    w_rows = width // n_plane
    b_at = gw_out.shape[1]

    def at_row(offset):
        return {"row": lax.rem(row + offset + n_row, n_row)}

    low, high = lax.rem(row, low_n), row // low_n
    place_id = low * n_col + col

    def in_plane(offset):
        q = lax.rem(place_id + offset, n_plane)
        return q, {"row": high * low_n + q // n_col, "col": lax.rem(q, n_col)}

    def across(offset):
        return {"row": lax.rem(high + offset, high_n) * low_n + low}

    def clamp(index):
        return jnp.minimum(jnp.maximum(index, 0), half)

    def at_col(offset):
        return {"col": lax.rem(col + offset, n_col)}

    barrier = pltpu.get_barrier_semaphore()
    partners = (
        [at_row(o) for o in OFFSETS]
        + [in_plane(o)[1] for o in range(1, n_plane)]
        + [across(o) for o in range(1, high_n)]
    )
    for partner in partners:
        pl.semaphore_signal(barrier, inc=1, device_id=partner, device_id_type=MESH)

    small = [
        pltpu.make_async_copy(a, b, in_sem.at[n])
        for n, (a, b) in enumerate(
            [
                (dst, dst_v),
                (src, src_v),
                (features, feat_w.at[pl.ds(BAND * node_dev, node_dev)]),
                (weight, wt_v),
                (bias, bias_v),
                (grad_out, go_v),
            ]
        )
    ]
    for copy in small[:2]:
        copy.start()
    loads = []
    for g in range(CHUNKS):
        for h in range(CHAINS):
            at = pl.ds(h * half + g * group, group)
            copy = pltpu.make_async_copy(tiles.at[0, at], tiles_v.at[at], tile_sem.at[g * CHAINS + h])
            copy.start()
            loads.append(copy)
    for copy in small[2:]:
        copy.start()

    small[0].wait()
    small[1].wait()
    lane = lax.broadcasted_iota(jnp.int32, (1, maxt), 1)
    key = jnp.where(lane < count[0], dst_v[...] * window_tiles + src_v[...], -1).astype(F32)
    key = jnp.broadcast_to(key, (maxt, maxt))
    key_t = key.T
    ri = lax.broadcasted_iota(jnp.int32, (maxt, maxt), 0)
    ci = lax.broadcasted_iota(jnp.int32, (maxt, maxt), 1)
    ri_f = ri.astype(F32)
    prev = jnp.zeros((maxt, maxt), F32)
    for h in range(CHAINS):
        inside = (ri >= h * half) & (ri < ci) & (ci < (h + 1) * half)
        prev = jnp.where((key == key_t) & inside, ri_f + (1.0 - h * half), prev)
    idx_v[0:1, 0:maxt] = jnp.max(prev, 0, keepdims=True).astype(jnp.int32)
    pairs = idx_v.shape[1]
    key_c = jnp.broadcast_to(key_t[:, 0:1], (maxt, pairs))
    pc = lax.broadcasted_iota(jnp.int32, (maxt, pairs), 1).astype(F32)
    pr = lax.broadcasted_iota(jnp.int32, (maxt, pairs), 0)
    for h in range(CHAINS):
        inside = (pr >= h * half) & (pr < (h + 1) * half)
        last = jnp.where((key_c == pc) & inside, pr.astype(F32) + (1.0 - h * half), 0.0)
        idx_v[h + 1 : h + 2, :] = jnp.max(last, 0, keepdims=True).astype(jnp.int32)
    to_scalar = pltpu.make_async_copy(idx_v, idx_s, idx_sem)
    to_scalar.start()

    pl.semaphore_wait(barrier, len(partners))
    halos = []
    for n, o in enumerate(OFFSETS):
        copy = pltpu.make_async_remote_copy(
            src_ref=features,
            dst_ref=feat_w.at[pl.ds((o + BAND) * node_dev, node_dev)],
            send_sem=halo_s.at[n],
            recv_sem=halo_r.at[n],
            device_id=at_row(-o),
            device_id_type=MESH,
        )
        copy.start()
        halos.append(copy)

    for h in range(CHAINS):
        sums[h, 0] = jnp.zeros((tile, tile), F32)
    to_scalar.wait()
    for g in range(CHUNKS):
        for h in range(CHAINS):
            loads[g * CHAINS + h].wait()

        def add(i, carry):
            slot = g * group + i
            for h in range(CHAINS):
                before = clamp(idx_s[0, h * half + slot])
                sums[h, slot + 1] = tiles_v[h * half + slot].astype(F32) + sums[h, before]
            return carry

        lax.fori_loop(0, group, add, 0, unroll=2)

    def place(j, carry):
        cols = pl.ds(pl.multiple_of(j * tile, tile), tile)
        for d in range(dst_tiles):
            total = sums[0, clamp(idx_s[1, d * window_tiles + j])]
            for h in range(1, CHAINS):
                total = total + sums[h, clamp(idx_s[h + 1, d * window_tiles + j])]
            adj[pl.ds(d * tile, tile), cols] = total.astype(BF16)
            adj_t[cols, pl.ds(d * tile, tile)] = total.T.astype(BF16)
        return carry

    lax.fori_loop(0, window_tiles, place, 0)

    for copy in small[2:]:
        copy.wait()

    def window_part(o):
        at = pl.ds((o + BAND) * node_dev, node_dev)
        return dot(adj[:, at], feat_w[at, :], ((1,), (0,)))

    acc[...] = window_part(0)
    for n, o in sorted(enumerate(OFFSETS), key=lambda p: abs(p[1])):
        halos[n].wait_recv()
        acc[...] += window_part(o)
    part[...] = acc[...].astype(BF16)

    mine = pl.ds(pl.multiple_of(col * node_dev, node_dev), node_dev)
    sends = []
    for o in range(1, n_col):
        q = lax.rem(col + o, n_col)
        copy = pltpu.make_async_remote_copy(
            src_ref=part.at[pl.ds(pl.multiple_of(q * node_dev, node_dev), node_dev)],
            dst_ref=part_in.at[col],
            send_sem=part_s.at[o - 1],
            recv_sem=part_r.at[o - 1],
            device_id=at_col(o),
            device_id_type=MESH,
        )
        copy.start()
        sends.append(copy)
    part_in[col] = part[mine, :]
    for copy in sends:
        copy.wait_recv()
    summed = part_in[0].astype(F32)
    for q in range(1, n_col):
        summed = summed + part_in[q].astype(F32)
    agg_v[...] = summed.astype(BF16)

    pre = dot(agg_v[...], wt_v[...], ((1,), (0,))) + bias_v[...]
    sig = jax.nn.sigmoid(pre)
    act_v[...] = (pre * sig).astype(BF16)
    dpre_v[...] = (go_v[...].astype(F32) * sig * (1.0 + pre * (1.0 - sig))).astype(BF16)
    w_term = dot(agg_v[...], dpre_v[...], ((0,), (0,))).astype(BF16)
    b_term = jnp.sum(dpre_v[...].astype(F32), 0, keepdims=True).astype(BF16)
    for q in range(n_plane):
        pay[q, 0:w_rows, :] = w_term[q * w_rows : (q + 1) * w_rows, :]
        pay[q, b_at:, :] = jnp.broadcast_to(b_term, (pay_rows - b_at, b_term.shape[1]))
    pays = []
    for o in range(1, n_plane):
        q, target = in_plane(o)
        copy = pltpu.make_async_remote_copy(
            src_ref=pay.at[q],
            dst_ref=pay_in.at[place_id],
            send_sem=pay_s.at[o - 1],
            recv_sem=pay_r.at[o - 1],
            device_id=target,
            device_id_type=MESH,
        )
        copy.start()
        pays.append(copy)
    pay_in[place_id] = pay[place_id]

    grads[mine, :] = dot(dpre_v[...], wt_v[...], ((1,), (1,))).astype(BF16)
    gathers = []
    for o in range(1, n_col):
        copy = pltpu.make_async_remote_copy(
            src_ref=grads.at[mine],
            dst_ref=grads.at[mine],
            send_sem=ga_s.at[o - 1],
            recv_sem=ga_r.at[o - 1],
            device_id=at_col(o),
            device_id_type=MESH,
        )
        copy.start()
        gathers.append(copy)
    act_copy = pltpu.make_async_copy(act_v, act_out, out_sem.at[0])
    act_copy.start()

    for copy in gathers:
        copy.wait_recv()

    def back_part(o):
        return dot(adj_t[pl.ds((o + BAND) * node_dev, node_dev), :], grads[...], ((1,), (0,)))

    backs = []
    for n, o in list(enumerate(OFFSETS))[:2]:
        back[n] = back_part(o).astype(BF16)
        copy = pltpu.make_async_remote_copy(
            src_ref=back.at[n],
            dst_ref=back_in.at[n],
            send_sem=bk_s.at[n],
            recv_sem=bk_r.at[n],
            device_id=at_row(o),
            device_id_type=MESH,
        )
        copy.start()
        backs.append(copy)

    for copy in pays:
        copy.wait_recv()
    value = pay_in[0].astype(F32)
    for q in range(1, n_plane):
        value = value + pay_in[q].astype(F32)
    bf_in[high] = value.astype(BF16)
    flips = []
    for o in range(1, high_n):
        copy = pltpu.make_async_remote_copy(
            src_ref=bf_in.at[high],
            dst_ref=bf_in.at[high],
            send_sem=bf_s.at[o - 1],
            recv_sem=bf_r.at[o - 1],
            device_id=across(o),
            device_id_type=MESH,
        )
        copy.start()
        flips.append(copy)
    for n, o in list(enumerate(OFFSETS))[2:]:
        back[n] = back_part(o).astype(BF16)
        copy = pltpu.make_async_remote_copy(
            src_ref=back.at[n],
            dst_ref=back_in.at[n],
            send_sem=bk_s.at[n],
            recv_sem=bk_r.at[n],
            device_id=at_row(o),
            device_id_type=MESH,
        )
        copy.start()
        backs.append(copy)

    acc[0:node_dev, :] = back_part(0)
    for copy in flips:
        copy.wait_recv()
    value = bf_in[0].astype(F32)
    for q in range(1, high_n):
        value = value + bf_in[q].astype(F32)
    gw_v[place_id] = value[0:b_at, :].astype(BF16)
    ends = []
    for o in range(1, n_plane):
        copy = pltpu.make_async_remote_copy(
            src_ref=gw_v.at[place_id],
            dst_ref=gw_v.at[place_id],
            send_sem=ag_s.at[o - 1],
            recv_sem=ag_r.at[o - 1],
            device_id=in_plane(o)[1],
            device_id_type=MESH,
        )
        copy.start()
        ends.append(copy)
    gb_v[...] = value[b_at : b_at + 1, :]
    gb_copy = pltpu.make_async_copy(gb_v, gb_out, out_sem.at[3])
    gb_copy.start()

    for copy in backs:
        copy.wait_recv()
    total = acc[0:node_dev, :]
    for n in range(len(OFFSETS)):
        total = total + back_in[n].astype(F32)
    gf_v[...] = total.astype(BF16)
    gf_copy = pltpu.make_async_copy(gf_v, gf_out, out_sem.at[1])
    gf_copy.start()
    for copy in ends:
        copy.wait_recv()
    gw_copy = pltpu.make_async_copy(gw_v, gw_out, out_sem.at[2])
    gw_copy.start()
    for copy in halos + sends + gathers + pays + backs + flips + ends:
        copy.wait_send()
    for copy in (act_copy, gf_copy, gb_copy, gw_copy):
        copy.wait()


def finish(scale, act_in, gf_in, gw_in, gb_in, act_out, gf_out, gw_out, gb_out):
    act_out[...] = act_in[...]
    gf_out[...] = gf_in[...]
    rows = gw_out.shape[0] // gw_in.shape[0]
    for q in range(gw_in.shape[0]):
        gw_out[q * rows : (q + 1) * rows, :] = gw_in[q, 0:rows, :].astype(F32) * (1.0 / scale)
    gb_out[...] = gb_in[...] * (1.0 / scale)


def local(n_row, n_col, features, weight, bias, grad_out, tiles, tile_count, tile_dst, tile_src):
    node_dev, width = features.shape
    hidden = weight.shape[1]
    maxt, tile = tiles.shape[1], tiles.shape[2]
    window = (2 * BAND + 1) * node_dev
    nodes = n_col * node_dev
    pairs = (nodes // tile) * (window // tile)
    pairs = max(-(-pairs // 128) * 128, maxt)
    low_n = math.isqrt(n_row)
    while n_row % low_n:
        low_n -= 1
    high_n = n_row // low_n
    n_plane = low_n * n_col
    b_at = -(-(width // n_plane) // 8) * 8
    pay_rows = b_at + 8
    offs = len(OFFSETS)
    dma = pltpu.SemaphoreType.DMA
    any_spec = pl.BlockSpec(memory_space=pl.ANY)
    out = pl.pallas_call(
        functools.partial(kernel, n_row, n_col),
        out_shape=(
            jax.ShapeDtypeStruct((node_dev, hidden), BF16),
            jax.ShapeDtypeStruct((node_dev, width), BF16),
            jax.ShapeDtypeStruct((n_plane, b_at, hidden), BF16),
            jax.ShapeDtypeStruct((1, hidden), F32),
        ),
        in_specs=[any_spec] * 5 + [pl.BlockSpec(memory_space=pltpu.SMEM)] + [any_spec] * 2,
        out_specs=(any_spec,) * 4,
        scratch_shapes=[
            pltpu.VMEM((maxt, tile, tile), BF16),
            pltpu.VMEM((CHAINS, maxt // CHAINS + 1, tile, tile), F32),
            pltpu.VMEM((window, width), BF16),
            pltpu.VMEM((width, hidden), BF16),
            pltpu.VMEM((1, hidden), F32),
            pltpu.VMEM((node_dev, hidden), BF16),
            pltpu.VMEM((1, maxt), jnp.int32),
            pltpu.VMEM((1, maxt), jnp.int32),
            pltpu.VMEM((8, pairs), jnp.int32),
            pltpu.SMEM((8, pairs), jnp.int32),
            pltpu.VMEM((nodes, window), BF16),
            pltpu.VMEM((window, nodes), BF16),
            pltpu.VMEM((nodes, width), F32),
            pltpu.VMEM((nodes, width), BF16),
            pltpu.VMEM((n_col, node_dev, width), BF16),
            pltpu.VMEM((node_dev, width), BF16),
            pltpu.VMEM((node_dev, hidden), BF16),
            pltpu.VMEM((node_dev, hidden), BF16),
            pltpu.VMEM((nodes, width), BF16),
            pltpu.VMEM((offs, node_dev, width), BF16),
            pltpu.VMEM((offs, node_dev, width), BF16),
            pltpu.VMEM((node_dev, width), BF16),
            pltpu.VMEM((n_plane, pay_rows, hidden), BF16),
            pltpu.VMEM((n_plane, pay_rows, hidden), BF16),
            pltpu.VMEM((high_n, pay_rows, hidden), BF16),
            pltpu.VMEM((n_plane, b_at, hidden), BF16),
            pltpu.VMEM((1, hidden), F32),
            dma((CHAINS * CHUNKS,)),
            dma((6,)),
            dma(()),
            dma((4,)),
        ]
        + [
            dma((n,))
            for n in (offs, n_col - 1, n_col - 1, offs, n_plane - 1, high_n - 1, n_plane - 1)
            for _ in range(2)
        ],
        compiler_params=pltpu.CompilerParams(
            collective_id=0, has_side_effects=True, vmem_limit_bytes=60 * 1024 * 1024
        ),
        name="graph_conv",
    )(features, weight, bias.reshape(1, hidden), grad_out, tiles, tile_count, tile_dst, tile_src)
    vmem = pl.BlockSpec(memory_space=pltpu.VMEM)
    out = pl.pallas_call(
        functools.partial(finish, math.sqrt(node_dev * n_row * n_col)),
        out_shape=(
            jax.ShapeDtypeStruct((node_dev, hidden), BF16),
            jax.ShapeDtypeStruct((node_dev, width), BF16),
            jax.ShapeDtypeStruct((width, hidden), F32),
            jax.ShapeDtypeStruct((1, hidden), F32),
        ),
        in_specs=[vmem] * 4,
        out_specs=(vmem,) * 4,
        name="finish",
    )(*out)
    return out[0], out[1], out[2], out[3].reshape(hidden)


def solution(mesh):
    in_specs = (
        P(("row", "col"), None),
        P(),
        P(),
        P(("row", "col"), None),
        P(("row", "col"), None, None, None),
        P(("row", "col")),
        P(("row", "col"), None),
        P(("row", "col"), None),
    )
    out_specs = (P(("row", "col"), None), P(("row", "col"), None), P(), P())
    body = functools.partial(local, mesh.shape["row"], mesh.shape["col"])
    return jax.shard_map(body, mesh=mesh, in_specs=in_specs, out_specs=out_specs, check_vma=False)
```
